32 devices in a mesh: front: 4 (over x, core), wide: 4 (over z), narrow: 2 (over y).
Axes of the slice: x: 2, y: 2, z: 4, core: 2. Of those that a mesh axis runs over, the one named last changes fastest.
Arguments:
- boundary: int32 [8, 32], P('front'), may hold values from 0 to 63, as said below
- owner: int32 [64], replicated, may hold values from 0 to 1, as said below
- ancestor_cov: bfloat16 [64, 128, 8192], P('narrow', None, 'wide'), may hold values from -1 to 3, as said below
- gain: bfloat16 [8, 4096, 2048], P('front', 'narrow', 'wide'), may hold values from -0.59765625 to 0.59765625
- pivot_inverse: float32 [8, 2048, 256], P('front', 'narrow', 'wide'), may hold values from -6 to 6
Outputs:
- boundary_cov: float32 [8, 2048, 4096], P('front', 'narrow', 'wide')
- diag_cov: float32 [8, 2048, 256], P('front', 'narrow', 'wide')
The draws below stay inside these ranges and needn't reach their ends.
Inputs may be any that keep to these rules, and one draw needn't show every extreme that they name: `boundary`: each row lists 32 distinct ancestor blocks; for every w below 4, positions w * 8 to (w + 1) * 8 - 1 hold blocks from w * 16 to (w + 1) * 16 - 1; for every n below 2, positions n * 16 to (n + 1) * 16 - 1 hold at most 8 blocks of one owner. In every aligned group of 2 block rows each narrow index owns exactly one; every narrow index owns 32 block rows, and block row r sits in that owner's slot r // 2. `ancestor_cov`: the ancestors' covariance that it holds is symmetric.
All inputs are finite; a program needn't handle non-finite values.
Results may differ from the reference program's by a relative error of at most 0.014.
Values may be sent and summed in bfloat16 or wider, within the bound.
A program may use at most 128 MiB of HBM per device.

```python
import jax
import jax.numpy as jnp
from jax import lax

BLK = 128
NB = 4096
NP = 2048
IMG = 256
ANC_BLK = 64
FRONTS = 8
NBB = 32
N_WIDE = 4
N_NARROW = 2


def owner_table(key):
    groups = ANC_BLK // N_NARROW
    base_key = jax.random.fold_in(key, 7)

    def one_group(index):
        return jax.random.permutation(jax.random.fold_in(base_key, index), N_NARROW).astype(jnp.int32)
    return jax.vmap(one_group)(jnp.arange(groups, dtype=jnp.int32))


def draw_owner(key, part):
    table = owner_table(key)
    rows = jnp.arange(ANC_BLK, dtype=jnp.int32)
    return table[rows // N_NARROW, rows % N_NARROW].astype(jnp.int32)


def draw_boundary(key, part):
    base_key = jax.random.fold_in(key, 23)
    rows_each = NB // (BLK * N_WIDE)
    range_blocks = ANC_BLK // N_WIDE
    picks_range = range_blocks // rows_each
    classes = (rows_each + N_NARROW - 1) // N_NARROW

    def one_front(member):
        front_key = jax.random.fold_in(base_key, member)
        class_steps = jax.random.randint(jax.random.fold_in(front_key, 1), (N_WIDE, classes), 0, picks_range)
        within = jnp.arange(rows_each, dtype=jnp.int32)[None, :]
        steps_taken = jnp.take(class_steps, jnp.arange(rows_each, dtype=jnp.int32) // N_NARROW, axis=1)
        offsets = within + rows_each * steps_taken
        scores = jax.random.randint(jax.random.fold_in(front_key, 2), (N_WIDE, rows_each), 0, 1 << 20) * rows_each + within
        order = jnp.argsort(scores, axis=1)
        offsets = jnp.take_along_axis(offsets, order, axis=1)
        blocks = offsets + (jnp.arange(N_WIDE, dtype=jnp.int32) * range_blocks)[:, None]
        return blocks.reshape(-1).astype(jnp.int32)
    return jax.vmap(one_front)(jnp.arange(FRONTS, dtype=jnp.int32))


def draw_ancestor_cov(key, part):
    table = owner_table(key)
    full_order = ANC_BLK * BLK
    base_key = jax.random.fold_in(key, 41)
    spread = 0.35 / full_order ** 0.5
    noise = jax.random.normal(jax.random.fold_in(base_key, 1), (full_order, full_order), jnp.float32)
    diagonal = jax.random.uniform(jax.random.fold_in(base_key, 2), (full_order,), jnp.float32, 1.2, 2.0)
    matrix = (noise + jnp.transpose(noise)) * spread
    places = jnp.arange(full_order)
    matrix = matrix.at[places, places].add(diagonal)
    per_owner = ANC_BLK // N_NARROW
    inverse_table = jnp.argsort(table, axis=1).astype(jnp.int32)
    slot_ids = jnp.arange(ANC_BLK, dtype=jnp.int32)
    holder = slot_ids // per_owner
    group = slot_ids % per_owner
    block_row = group * N_NARROW + inverse_table[group, holder]
    return jnp.take(matrix.reshape(ANC_BLK, BLK, full_order), block_row, axis=0).astype(jnp.bfloat16)


def shard_levels(rng, extent, cuts, low, top_value):
    level, own = 1.0, jax.random.fold_in(rng, 6)
    for axis_at, parts in cuts:
        heights = jnp.exp(jax.random.uniform(jax.random.fold_in(own, axis_at), (parts,), jnp.float32, low / len(cuts), top_value / len(cuts)))
        level = level * jnp.repeat(heights, extent[axis_at] // parts).reshape([-1 if axis == axis_at else 1 for axis in range(len(extent))])
    return level


def centred(key, shape, width, most, split=(), kind=jnp.bfloat16):
    factor_of = shard_levels(key, shape, split, -0.22, 0.18) if split else 1.0
    entries = jax.random.normal(key, shape, jnp.float32) * width * factor_of
    return jnp.minimum(jnp.maximum(entries, -most), most).astype(kind)


def setup_inputs(seed: int = 0) -> dict:
    seeds = jax.random.split(jax.random.key(seed), 6)
    return {
        "boundary": draw_boundary(jax.random.fold_in(seeds[5], 71), 0),
        "owner": draw_owner(jax.random.fold_in(seeds[5], 71), 0),
        "ancestor_cov": draw_ancestor_cov(jax.random.fold_in(seeds[5], 71), 0),
        "gain": centred(seeds[3], (FRONTS, NB, NP), 0.08, 0.59765625, ((0, 4), (1, 2), (2, 4))),
        "pivot_inverse": centred(seeds[4], (FRONTS, NP, IMG), 1.0, 6.0, ((0, 4), (1, 2), (2, 4)), jnp.float32),
    }


def front_result(inputs, owner, ancestor_cov):
    boundary_set, gain_panel, pivot_block = inputs
    per_owner = ANC_BLK // N_NARROW
    slot_of = owner * per_owner + jnp.arange(ANC_BLK, dtype=jnp.int32) // N_NARROW
    rows_taken = jnp.take(ancestor_cov, slot_of[boundary_set], axis=0)
    reshaped = rows_taken.reshape(NBB, BLK, ANC_BLK, BLK)
    coupling = jnp.take(reshaped, boundary_set, axis=2).reshape(NB, NB)
    blocks_each = NBB // N_NARROW
    total = jnp.zeros((NB, NP), jnp.float32)
    for narrow in range(N_NARROW):
        start = narrow * blocks_each * BLK
        width_rows = blocks_each * BLK
        partial_value = jnp.dot(lax.dynamic_slice_in_dim(coupling, start, width_rows, 1),
                          lax.dynamic_slice_in_dim(gain_panel, start, width_rows, 0),
                          preferred_element_type=jnp.float32)
        rounded = lax.optimization_barrier(partial_value.astype(jnp.bfloat16))
        total = total + rounded.astype(jnp.float32)
    cross_cov = -jnp.transpose(total)
    cross_low = cross_cov.astype(jnp.bfloat16)
    site_count = NP // IMG
    left_side = cross_low.reshape(site_count, IMG, NB).astype(jnp.float32)
    right_side = gain_panel.reshape(NB, site_count, IMG).astype(jnp.float32)
    blocks_out = jnp.einsum("ipr,riq->ipq", left_side, right_side)
    diag_cov = pivot_block - blocks_out.reshape(NP, IMG)
    return cross_cov, diag_cov


def reference(boundary, owner, ancestor_cov, gain, pivot_inverse):
    def one_front(inputs):
        return front_result(inputs, owner, ancestor_cov)

    boundary_cov, diag_cov = lax.map(one_front, (boundary, gain, pivot_inverse))
    return boundary_cov, diag_cov
```

```python
import functools

import jax
import jax.numpy as jnp
from jax import lax
from jax.experimental import pallas as pl
from jax.experimental.pallas import tpu as pltpu
from jax.sharding import PartitionSpec as P

BLK = 128
IMG = 256


def slot_plan(boundary_set, owner, source, n_narrow, blocks_each, capacity):
    positions = boundary_set.reshape(n_narrow, blocks_each)
    holders = owner[positions]
    owned_mask = (holders == source).astype(jnp.int32)
    rank_of = jnp.cumsum(owned_mask, axis=1) - 1
    slot_ids = jnp.arange(capacity, dtype=jnp.int32)
    picked = owned_mask[:, None, :] * (rank_of[:, None, :] == slot_ids[None, :, None]).astype(
        jnp.int32
    )
    local_slot = jnp.sum(picked * (positions // n_narrow)[:, None, :], axis=2)
    is_valid = jnp.sum(picked, axis=2)
    return (local_slot, is_valid)


def column_panel(ancestor_cov, boundary_set, wide_index, rows_each, range_blocks):
    col_blocks = (
        lax.dynamic_slice_in_dim(boundary_set, wide_index * rows_each, rows_each)
        - wide_index * range_blocks
    )
    reshaped = ancestor_cov.reshape(ancestor_cov.shape[0], BLK, range_blocks, BLK)
    picked = jnp.take(reshaped, col_blocks, axis=2)
    return picked.reshape(ancestor_cov.shape[0], BLK, rows_each * BLK)


def arrange(arrived, boundary_set, owner, narrow, blocks_each, capacity):
    positions = lax.dynamic_slice_in_dim(boundary_set, narrow * blocks_each, blocks_each)
    holders = owner[positions]
    matches = (holders[:, None] == holders[None, :]).astype(jnp.int32)
    rank_of = jnp.sum(jnp.tril(matches, -1), axis=1)
    flattened = arrived.reshape((-1,) + arrived.shape[2:])
    chosen = jnp.take(flattened, holders * capacity + rank_of, axis=0)
    return chosen.reshape(blocks_each * chosen.shape[1], chosen.shape[2])


def local(boundary, owner, ancestor_cov, gain, pivot_inverse):
    n_wide = lax.axis_size("wide")
    n_narrow = lax.axis_size("narrow")
    wide_index = lax.axis_index("wide")
    narrow = lax.axis_index("narrow")
    fronts, blocks = boundary.shape
    rows_each = blocks // n_wide
    blocks_each = blocks // n_narrow
    range_blocks = ancestor_cov.shape[2] // BLK
    capacity = max(1, blocks_each // n_narrow)
    pivots = gain.shape[2] * n_wide
    pivots_here = pivots // n_narrow
    site_count = pivots_here // IMG
    results = []
    for member in range(fronts):
        local_slot, is_valid = slot_plan(
            boundary[member], owner, narrow, n_narrow, blocks_each, capacity
        )
        row_panel = column_panel(
            ancestor_cov, boundary[member], wide_index, rows_each, range_blocks
        )
        rows_out = jnp.take(row_panel, local_slot.reshape(-1), axis=0)
        rows_out = rows_out.reshape(n_narrow, capacity, BLK, rows_each * BLK)
        arrived = lax.all_to_all(
            jnp.where(
                is_valid.reshape(n_narrow, capacity, 1, 1) > 0, rows_out, jnp.zeros_like(rows_out)
            ),
            "narrow",
            split_axis=0,
            concat_axis=0,
            tiled=True,
        )
        coupling = arrange(arrived, boundary[member], owner, narrow, blocks_each, capacity)
        gathered = lax.all_gather(gain[member], "wide", axis=1, tiled=True)
        summed = lax.psum_scatter(
            lax.dot_general(
                gathered, coupling, (((0,), (0,)), ((), ())), preferred_element_type=jnp.float32
            ).astype(jnp.bfloat16),
            "narrow",
            scatter_dimension=0,
            tiled=True,
        ).astype(jnp.float32)
        cross_cov = -summed
        root_index = wide_index * rows_each // blocks_each
        offset = (
            jnp.clip(wide_index * rows_each - narrow * blocks_each, 0, blocks_each - rows_each)
            * BLK
        )
        own_rows = lax.dynamic_slice_in_dim(gathered, offset, rows_each * BLK, 0)
        pieces = jnp.transpose(own_rows.reshape(rows_each * BLK, n_narrow, pivots_here), (1, 0, 2))
        arrived_pieces = lax.all_to_all(pieces, "narrow", split_axis=0, concat_axis=0, tiled=True)
        gain_here = lax.dynamic_index_in_dim(arrived_pieces, root_index, 0, keepdims=False)
        cross_low = cross_cov.astype(jnp.bfloat16)
        left_side = cross_low.reshape(site_count, IMG, rows_each * BLK)
        right_side = gain_here.reshape(rows_each * BLK, site_count, IMG)
        blocks_out = jnp.einsum(
            "ipr,riq->ipq", left_side, right_side, preferred_element_type=jnp.float32
        )
        partial_value = blocks_out.reshape(pivots_here, IMG)
        reduced = lax.psum_scatter(
            partial_value.astype(jnp.bfloat16), "wide", scatter_dimension=1, tiled=True
        ).astype(jnp.float32)
        results.append((cross_cov, pivot_inverse[member] - reduced))
    boundary_cov = jnp.stack([pair[0] for pair in results])
    diag_cov = jnp.stack([pair[1] for pair in results])
    return (boundary_cov, diag_cov)


MESH = pl.DeviceIdType.MESH
NT = (((1,), (1,)), ((), ()))


def pick_kernel(
    fronts, half_blocks, cols_each,
    slot_ref, col_ref, take_ref, cov_ref, gain_ref, tile_ref, pack_ref,
    tiles, raw, turned, tile_in, raw_in, tile_out, pack_out,
):
    per_front = 2 * half_blocks
    lines = fronts * per_front

    def fetch_gain(line, carry):
        f = line // per_front
        at = f * per_front + take_ref[f, lax.rem(line, per_front)]
        pltpu.make_async_copy(gain_ref.at[at], raw.at[line], raw_in.at[line]).start()
        return carry

    def fetch_tile(line, carry):
        f = line // per_front
        slot = slot_ref[f, lax.rem(line, per_front)]
        for c in range(cols_each):
            col = pl.multiple_of(col_ref[f, c], BLK)
            pltpu.make_async_copy(
                cov_ref.at[slot, :, pl.ds(col, BLK)],
                tiles.at[line, :, pl.ds(c * BLK, BLK)],
                tile_in.at[line],
            ).start()
        return carry

    def turn(group, carry):
        for r in range(half_blocks):
            line = group * half_blocks + r
            pltpu.make_async_copy(raw.at[line], raw.at[line], raw_in.at[line]).wait()
            turned[group, :, r * BLK : (r + 1) * BLK] = raw[line].T
        pltpu.make_async_copy(turned.at[group], pack_ref.at[group], pack_out.at[group]).start()
        return carry

    def store_tile(line, carry):
        pltpu.make_async_copy(tiles.at[line], tiles.at[line], tile_in.at[line]).wait()
        pltpu.make_async_copy(tiles.at[line], tile_ref.at[line], tile_out.at[line]).start()
        return carry

    def finish_tile(line, carry):
        pltpu.make_async_copy(tiles.at[line], tile_ref.at[line], tile_out.at[line]).wait()
        return carry

    def finish_pack(group, carry):
        pltpu.make_async_copy(turned.at[group], pack_ref.at[group], pack_out.at[group]).wait()
        return carry

    lax.fori_loop(0, lines, fetch_gain, 0)
    lax.fori_loop(0, lines, fetch_tile, 0)
    lax.fori_loop(0, fronts * 2, turn, 0)
    lax.fori_loop(0, lines, store_tile, 0)
    lax.fori_loop(0, lines, finish_tile, 0)
    lax.fori_loop(0, fronts * 2, finish_pack, 0)


def fused_kernel(
    fronts, half_blocks, cols_each, n_sites,
    pick_ref, gain_ref, tile_ref,
    own_ref, got_ref, diag_ref,
    tile, picked, panels, prods, got, kept, d_out, d_in, parts, parts_in,
    tile_sem, own_sem, ex_send, ex_recv, side_send, side_recv, fwd_send, fwd_recv,
    rs_send, rs_recv, d_send, d_recv, e_send, e_recv, put_sem, keep_sem,
):
    n_wide = lax.axis_size("wide")
    n_narrow = lax.axis_size("narrow")
    w = lax.axis_index("wide")
    n = lax.axis_index("narrow")
    right = lax.rem(w + 1, n_wide)
    left = lax.rem(w + n_wide - 1, n_wide)
    partner = 1 - n
    shards_each = n_wide // n_narrow
    width = panels.shape[3]
    site_rows = width // IMG
    slice_rows = IMG // n_wide
    half = width // 2

    tile_copy = pltpu.make_async_copy(tile_ref, tile, tile_sem)
    tile_copy.start()
    own_copies = []
    for f in range(fronts):
        own_copies.append(
            pltpu.make_async_copy(gain_ref.at[f, 0], panels.at[f, 0, 0], own_sem.at[f])
        )
        own_copies[-1].start()

    barrier = pltpu.get_barrier_semaphore()
    for step in range(1, n_wide):
        pl.semaphore_signal(
            barrier, inc=1, device_id={"wide": lax.rem(w + step, n_wide)}, device_id_type=MESH
        )
    pl.semaphore_signal(barrier, inc=1, device_id={"narrow": partner}, device_id_type=MESH)
    pl.semaphore_wait(barrier, n_wide)

    def exchange(f):
        return pltpu.make_async_remote_copy(
            src_ref=gain_ref.at[f, 1], dst_ref=panels.at[f, 0, 1],
            send_sem=ex_send.at[f], recv_sem=ex_recv.at[f],
            device_id={"narrow": partner}, device_id_type=MESH,
        )

    def side(f, h, way):
        return pltpu.make_async_remote_copy(
            src_ref=panels.at[f, 0, h], dst_ref=panels.at[f, 1 if way == 0 else n_wide - 1, h],
            send_sem=side_send.at[f, h, way], recv_sem=side_recv.at[f, h, way],
            device_id={"wide": right if way == 0 else left}, device_id_type=MESH,
        )

    def forward(f, h, way):
        rows = pl.ds(0 if way == 0 else half, half)
        return pltpu.make_async_remote_copy(
            src_ref=panels.at[f, 1 if way == 0 else n_wide - 1, h, rows],
            dst_ref=panels.at[f, 2, h, rows],
            send_sem=fwd_send.at[f, h, way], recv_sem=fwd_recv.at[f, h, way],
            device_id={"wide": right if way == 0 else left}, device_id_type=MESH,
        )

    def scatter(f, d, i):
        return pltpu.make_async_remote_copy(
            src_ref=prods.at[f, d], dst_ref=got.at[f, i],
            send_sem=rs_send.at[f, i], recv_sem=rs_recv.at[f, i],
            device_id={"narrow": partner}, device_id_type=MESH,
        )

    def keep(f, d, i):
        return pltpu.make_async_copy(prods.at[f, d], own_ref.at[f, i], keep_sem.at[f, i])

    def put(f, i):
        return pltpu.make_async_copy(got.at[f, i], got_ref.at[f, i], put_sem.at[f, i])

    def swap_sites(f):
        return pltpu.make_async_remote_copy(
            src_ref=d_out.at[f], dst_ref=d_in.at[f],
            send_sem=d_send.at[f], recv_sem=d_recv.at[f],
            device_id={"narrow": partner}, device_id_type=MESH,
        )

    def spread(f, step):
        to = lax.rem(w + step, n_wide)
        return pltpu.make_async_remote_copy(
            src_ref=parts.at[f, to], dst_ref=parts_in.at[f, step - 1],
            send_sem=e_send.at[f, step - 1], recv_sem=e_recv.at[f, step - 1],
            device_id={"wide": to}, device_id_type=MESH,
        )

    side_half = jnp.where(w // shards_each == n, 0, 1)

    def choose(f, d):
        def one(t, carry):
            rows = pl.ds(pl.multiple_of(t * BLK, BLK), BLK)
            blocks = [
                panels[f, d, side_half, rows, r * BLK : (r + 1) * BLK].astype(jnp.float32)
                for r in range(half_blocks)
            ]

            def column(j, inner):
                total = pick_ref[f, j, 0] * blocks[0]
                for r in range(1, half_blocks):
                    total += pick_ref[f, j, r] * blocks[r]
                picked[rows, pl.ds(pl.multiple_of(j * BLK, BLK), BLK)] = total.astype(jnp.bfloat16)
                return inner

            return lax.fori_loop(0, cols_each, column, carry)

        lax.fori_loop(0, width // BLK, one, 0)

    def site_product(left_ref, site):
        rows = pl.ds(pl.multiple_of(site * IMG, IMG), IMG)
        return lax.dot_general(
            left_ref[rows, :], picked[rows, :], NT, preferred_element_type=jnp.float32
        )

    col_step = 256

    def compute(f, d):
        s = lax.rem(w + n_wide - d, n_wide)
        i = lax.rem(s, shards_each)
        mine = s // shards_each == n

        def one(t, carry):
            cols = pl.ds(pl.multiple_of(t * col_step, col_step), col_step)
            total = jnp.dot(
                panels[f, d, 0], tile[f, 0, :, cols], preferred_element_type=jnp.float32
            ) + jnp.dot(panels[f, d, 1], tile[f, 1, :, cols], preferred_element_type=jnp.float32)
            prods[f, d, :, cols] = total.astype(jnp.bfloat16)
            return carry

        lax.fori_loop(0, cols_each * BLK // col_step, one, 0)

        @pl.when(mine)
        def _():
            keep(f, d, i).start()

        @pl.when(jnp.logical_not(mine))
        def _():
            scatter(f, d, i).start()

        choose(f, d)

        def one_site(site, carry):
            value = site_product(prods.at[f, d], site)

            @pl.when(mine)
            def _():
                kept[f, i * site_rows + site] = value

            @pl.when(jnp.logical_not(mine))
            def _():
                d_out[f, i * site_rows + site] = value.astype(jnp.bfloat16)

            return carry

        lax.fori_loop(0, site_rows, one_site, 0)

    def absorb(f, i):
        scatter(f, 0, i).wait_recv()
        put(f, i).start()
        d = lax.rem(w + n_wide - (n * shards_each + i), n_wide)

        choose(f, d)

        def one_site(site, carry):
            value = site_product(got.at[f, i], site)
            kept[f, i * site_rows + site] += value + value.T
            return carry

        lax.fori_loop(0, site_rows, one_site, 0)

    def fold(f):
        swap_sites(f).wait_recv()

        def one_site(site, carry):
            total = (kept[f, site] + d_in[f, site].astype(jnp.float32)).astype(jnp.bfloat16)
            for z in range(n_wide):
                parts[f, z, site] = total[z * slice_rows : (z + 1) * slice_rows]
            return carry

        lax.fori_loop(0, n_sites, one_site, 0)
        for step in range(1, n_wide):
            spread(f, step).start()

    for f in range(fronts):
        exchange(f).start()
    for copy in own_copies:
        copy.wait()
    for way in range(2):
        side(0, 0, way).start()
    tile_copy.wait()
    exchange(0).wait_recv()
    for way in range(2):
        side(0, 1, way).start()
    for f in range(fronts):
        for way in range(2):
            side(f, 0, way).wait_recv()
            forward(f, 0, way).start()
        compute(f, 0)
        for way in range(2):
            side(f, 1, way).wait_recv()
            forward(f, 1, way).start()
        if f + 1 < fronts:
            exchange(f + 1).wait_recv()
            for h in range(2):
                for way in range(2):
                    side(f + 1, h, way).start()
        compute(f, 1)
        compute(f, n_wide - 1)
        for h in range(2):
            for way in range(2):
                forward(f, h, way).wait_recv()
        compute(f, 2)
        swap_sites(f).start()
        if f > 0:
            for i in range(shards_each):
                absorb(f - 1, i)
            fold(f - 1)
    for i in range(shards_each):
        absorb(fronts - 1, i)
    fold(fronts - 1)

    for f in range(fronts):
        for step in range(1, n_wide):
            spread(f, step).wait_recv()
        total = parts[f, w].astype(jnp.float32)
        for step in range(1, n_wide):
            total += parts_in[f, step - 1].astype(jnp.float32)
        diag_ref[f] = total

    for f in range(fronts):
        exchange(f).wait_send()
        swap_sites(f).wait_send()
        for step in range(1, n_wide):
            spread(f, step).wait_send()
        for h in range(2):
            for way in range(2):
                side(f, h, way).wait_send()
                forward(f, h, way).wait_send()
        for i in range(shards_each):
            scatter(f, 0, i).wait_send()
            keep(f, 0, i).wait()
            put(f, i).wait()


def ranked(flags, count):
    at = jnp.cumsum(flags, axis=-1) - 1
    hit = flags[..., None, :] * (
        at[..., None, :] == jnp.arange(count, dtype=jnp.int32)[:, None]
    ).astype(jnp.int32)
    return jnp.sum(hit * jnp.arange(flags.shape[-1], dtype=jnp.int32), axis=-1)


def fused(boundary, owner, ancestor_cov, gain, pivot_inverse):
    n_wide = lax.axis_size("wide")
    n_narrow = lax.axis_size("narrow")
    w = lax.axis_index("wide")
    n = lax.axis_index("narrow")
    fronts, blocks = boundary.shape
    cols_each = blocks // n_wide
    blocks_each = blocks // n_narrow
    half_blocks = blocks_each // n_narrow
    range_blocks = ancestor_cov.shape[2] // BLK
    width = gain.shape[2]
    pivots_here = width * n_wide // n_narrow
    n_sites = pivots_here // IMG
    shards_each = n_wide // n_narrow
    slice_rows = IMG // n_wide
    bf16 = jnp.bfloat16

    holders = owner[boundary].reshape(fronts, n_narrow, blocks_each)
    own = (holders == n).astype(jnp.int32)
    places = ranked(own, half_blocks)
    mine_first = jnp.stack(
        [lax.dynamic_index_in_dim(places, n, 1, False), lax.dynamic_index_in_dim(places, 1 - n, 1, False) ],
        axis=1,
    )
    base = jnp.stack([n, 1 - n]).astype(jnp.int32)[None, :, None] * blocks_each
    at = (mine_first + base).reshape(fronts, 2 * half_blocks)
    slots = jnp.take_along_axis(boundary, at, axis=1) // n_narrow
    given = ranked(1 - lax.dynamic_index_in_dim(own, n, 1, False), half_blocks)
    take = jnp.concatenate([lax.dynamic_index_in_dim(places, n, 1, False), given], axis=1)
    columns = lax.dynamic_slice_in_dim(boundary, w * cols_each, cols_each, 1) - w * range_blocks
    columns = columns * BLK
    order = jnp.cumsum(own, axis=2) - 1
    order = order.reshape(fronts, blocks)
    ranks = lax.dynamic_slice_in_dim(order, w * cols_each, cols_each, 1)
    mask = lax.dynamic_slice_in_dim(own.reshape(fronts, blocks), w * cols_each, cols_each, 1)
    picks = mask[:, :, None] * (
        ranks[:, :, None] == jnp.arange(half_blocks, dtype=jnp.int32)
    ).astype(jnp.int32)
    picks = picks.astype(jnp.float32)

    rows = half_blocks * BLK
    cols = cols_each * BLK
    dma = pltpu.SemaphoreType.DMA
    smem = pl.BlockSpec(memory_space=pltpu.SMEM)
    anywhere = pl.BlockSpec(memory_space=pl.ANY)
    lines = fronts * 2 * half_blocks
    tile, packed = pl.pallas_call(
        functools.partial(pick_kernel, fronts, half_blocks, cols_each),
        out_shape=(
            jax.ShapeDtypeStruct((lines, BLK, cols), bf16),
            jax.ShapeDtypeStruct((fronts * 2, width, rows), bf16),
        ),
        in_specs=[smem] * 3 + [anywhere] * 2,
        out_specs=(anywhere, anywhere),
        scratch_shapes=[
            pltpu.VMEM((lines, BLK, cols), bf16),
            pltpu.VMEM((lines, BLK, width), bf16),
            pltpu.VMEM((fronts * 2, width, rows), bf16),
            dma((lines,)),
            dma((lines,)),
            dma((lines,)),
            dma((fronts * 2,)),
        ],
        compiler_params=pltpu.CompilerParams(vmem_limit_bytes=48 * 1024 * 1024),
    )(slots, columns, take, ancestor_cov, gain.reshape(lines, BLK, width))
    tile = tile.reshape(fronts, 2, rows, cols)
    packed = packed.reshape(fronts, 2, width, rows)
    piece = jax.ShapeDtypeStruct((fronts, shards_each, width, cols), bf16)
    kept_part, got_part, sites = pl.pallas_call(
        functools.partial(fused_kernel, fronts, half_blocks, cols_each, n_sites),
        out_shape=(
            piece,
            piece,
            jax.ShapeDtypeStruct((fronts, n_sites, slice_rows, IMG), jnp.float32),
        ),
        in_specs=[smem] + [anywhere] * 2,
        out_specs=(anywhere, anywhere, pl.BlockSpec(memory_space=pltpu.VMEM)),
        scratch_shapes=[
            pltpu.VMEM((fronts, 2, rows, cols), bf16),
            pltpu.VMEM((width, cols), bf16),
            pltpu.VMEM((fronts, n_wide, 2, width, rows), bf16),
            pltpu.VMEM((fronts, n_wide, width, cols), bf16),
            pltpu.VMEM((fronts, shards_each, width, cols), bf16),
            pltpu.VMEM((fronts, n_sites, IMG, IMG), jnp.float32),
            pltpu.VMEM((fronts, n_sites, IMG, IMG), bf16),
            pltpu.VMEM((fronts, n_sites, IMG, IMG), bf16),
            pltpu.VMEM((fronts, n_wide, n_sites, slice_rows, IMG), bf16),
            pltpu.VMEM((fronts, n_wide - 1, n_sites, slice_rows, IMG), bf16),
            dma,
            dma((fronts,)),
            dma((fronts,)),
            dma((fronts,)),
            dma((fronts, 2, 2)),
            dma((fronts, 2, 2)),
            dma((fronts, 2, 2)),
            dma((fronts, 2, 2)),
            dma((fronts, shards_each)),
            dma((fronts, shards_each)),
            dma((fronts,)),
            dma((fronts,)),
            dma((fronts, n_wide - 1)),
            dma((fronts, n_wide - 1)),
            dma((fronts, shards_each)),
            dma((fronts, shards_each)),
        ],
        compiler_params=pltpu.CompilerParams(
            collective_id=0, has_side_effects=True, vmem_limit_bytes=62 * 1024 * 1024
        ),
    )(picks, packed, tile)
    boundary_cov = -(kept_part.astype(jnp.float32) + got_part.astype(jnp.float32))
    boundary_cov = boundary_cov.reshape(fronts, pivots_here, cols)
    sums = jnp.swapaxes(sites, 2, 3).reshape(fronts, pivots_here, slice_rows)
    return (boundary_cov, pivot_inverse + sums)


def solution(mesh):
    placed = (
        P("front", None),
        P(),
        P("narrow", None, "wide"),
        P("front", "narrow", "wide"),
        P("front", "narrow", "wide"),
    )
    small = mesh.shape["wide"] == 4 and mesh.shape["narrow"] == 2
    return jax.shard_map(
        fused if small else local,
        mesh=mesh,
        in_specs=placed,
        out_specs=(P("front", "narrow", "wide"), P("front", "narrow", "wide")),
        check_vma=False,
    )
```

```python
import functools

import jax
import jax.numpy as jnp
from jax import lax
from jax.experimental import pallas as pl
from jax.experimental.pallas import tpu as pltpu
from jax.sharding import PartitionSpec as P

BLK = 128
IMG = 256


def slot_plan(boundary_set, owner, source, n_narrow, blocks_each, capacity):
    positions = boundary_set.reshape(n_narrow, blocks_each)
    holders = owner[positions]
    owned_mask = (holders == source).astype(jnp.int32)
    rank_of = jnp.cumsum(owned_mask, axis=1) - 1
    slot_ids = jnp.arange(capacity, dtype=jnp.int32)
    picked = owned_mask[:, None, :] * (rank_of[:, None, :] == slot_ids[None, :, None]).astype(
        jnp.int32
    )
    local_slot = jnp.sum(picked * (positions // n_narrow)[:, None, :], axis=2)
    is_valid = jnp.sum(picked, axis=2)
    return (local_slot, is_valid)


def column_panel(ancestor_cov, boundary_set, wide_index, rows_each, range_blocks):
    col_blocks = (
        lax.dynamic_slice_in_dim(boundary_set, wide_index * rows_each, rows_each)
        - wide_index * range_blocks
    )
    reshaped = ancestor_cov.reshape(ancestor_cov.shape[0], BLK, range_blocks, BLK)
    picked = jnp.take(reshaped, col_blocks, axis=2)
    return picked.reshape(ancestor_cov.shape[0], BLK, rows_each * BLK)


def arrange(arrived, boundary_set, owner, narrow, blocks_each, capacity):
    positions = lax.dynamic_slice_in_dim(boundary_set, narrow * blocks_each, blocks_each)
    holders = owner[positions]
    matches = (holders[:, None] == holders[None, :]).astype(jnp.int32)
    rank_of = jnp.sum(jnp.tril(matches, -1), axis=1)
    flattened = arrived.reshape((-1,) + arrived.shape[2:])
    chosen = jnp.take(flattened, holders * capacity + rank_of, axis=0)
    return chosen.reshape(blocks_each * chosen.shape[1], chosen.shape[2])


def local(boundary, owner, ancestor_cov, gain, pivot_inverse):
    n_wide = lax.axis_size("wide")
    n_narrow = lax.axis_size("narrow")
    wide_index = lax.axis_index("wide")
    narrow = lax.axis_index("narrow")
    fronts, blocks = boundary.shape
    rows_each = blocks // n_wide
    blocks_each = blocks // n_narrow
    range_blocks = ancestor_cov.shape[2] // BLK
    capacity = max(1, blocks_each // n_narrow)
    pivots = gain.shape[2] * n_wide
    pivots_here = pivots // n_narrow
    site_count = pivots_here // IMG
    results = []
    for member in range(fronts):
        local_slot, is_valid = slot_plan(
            boundary[member], owner, narrow, n_narrow, blocks_each, capacity
        )
        row_panel = column_panel(
            ancestor_cov, boundary[member], wide_index, rows_each, range_blocks
        )
        rows_out = jnp.take(row_panel, local_slot.reshape(-1), axis=0)
        rows_out = rows_out.reshape(n_narrow, capacity, BLK, rows_each * BLK)
        arrived = lax.all_to_all(
            jnp.where(
                is_valid.reshape(n_narrow, capacity, 1, 1) > 0, rows_out, jnp.zeros_like(rows_out)
            ),
            "narrow",
            split_axis=0,
            concat_axis=0,
            tiled=True,
        )
        coupling = arrange(arrived, boundary[member], owner, narrow, blocks_each, capacity)
        gathered = lax.all_gather(gain[member], "wide", axis=1, tiled=True)
        summed = lax.psum_scatter(
            lax.dot_general(
                gathered, coupling, (((0,), (0,)), ((), ())), preferred_element_type=jnp.float32
            ).astype(jnp.bfloat16),
            "narrow",
            scatter_dimension=0,
            tiled=True,
        ).astype(jnp.float32)
        cross_cov = -summed
        root_index = wide_index * rows_each // blocks_each
        offset = (
            jnp.clip(wide_index * rows_each - narrow * blocks_each, 0, blocks_each - rows_each)
            * BLK
        )
        own_rows = lax.dynamic_slice_in_dim(gathered, offset, rows_each * BLK, 0)
        pieces = jnp.transpose(own_rows.reshape(rows_each * BLK, n_narrow, pivots_here), (1, 0, 2))
        arrived_pieces = lax.all_to_all(pieces, "narrow", split_axis=0, concat_axis=0, tiled=True)
        gain_here = lax.dynamic_index_in_dim(arrived_pieces, root_index, 0, keepdims=False)
        cross_low = cross_cov.astype(jnp.bfloat16)
        left_side = cross_low.reshape(site_count, IMG, rows_each * BLK)
        right_side = gain_here.reshape(rows_each * BLK, site_count, IMG)
        blocks_out = jnp.einsum(
            "ipr,riq->ipq", left_side, right_side, preferred_element_type=jnp.float32
        )
        partial_value = blocks_out.reshape(pivots_here, IMG)
        reduced = lax.psum_scatter(
            partial_value.astype(jnp.bfloat16), "wide", scatter_dimension=1, tiled=True
        ).astype(jnp.float32)
        results.append((cross_cov, pivot_inverse[member] - reduced))
    boundary_cov = jnp.stack([pair[0] for pair in results])
    diag_cov = jnp.stack([pair[1] for pair in results])
    return (boundary_cov, diag_cov)


MESH = pl.DeviceIdType.MESH
NT = (((1,), (1,)), ((), ()))


def pick_kernel(
    fronts, half_blocks, cols_each,
    slot_ref, col_ref, take_ref, cov_ref, gain_ref, tile_ref, pack_ref,
    tiles, raw, turned, tile_in, raw_in, tile_out, pack_out,
):
    per_front = 2 * half_blocks
    lines = fronts * per_front

    def fetch_gain(line, carry):
        f = line // per_front
        at = f * per_front + take_ref[f, lax.rem(line, per_front)]
        pltpu.make_async_copy(gain_ref.at[at], raw.at[line], raw_in.at[line]).start()
        return carry

    def fetch_tile(line, carry):
        f = line // per_front
        slot = slot_ref[f, lax.rem(line, per_front)]
        for c in range(cols_each):
            col = pl.multiple_of(col_ref[f, c], BLK)
            pltpu.make_async_copy(
                cov_ref.at[slot, :, pl.ds(col, BLK)],
                tiles.at[line, :, pl.ds(c * BLK, BLK)],
                tile_in.at[line],
            ).start()
        return carry

    def turn(group, carry):
        for r in range(half_blocks):
            line = group * half_blocks + r
            pltpu.make_async_copy(raw.at[line], raw.at[line], raw_in.at[line]).wait()
            turned[group, :, r * BLK : (r + 1) * BLK] = raw[line].T
        pltpu.make_async_copy(turned.at[group], pack_ref.at[group], pack_out.at[group]).start()
        return carry

    def store_tile(line, carry):
        pltpu.make_async_copy(tiles.at[line], tiles.at[line], tile_in.at[line]).wait()
        pltpu.make_async_copy(tiles.at[line], tile_ref.at[line], tile_out.at[line]).start()
        return carry

    def finish_tile(line, carry):
        pltpu.make_async_copy(tiles.at[line], tile_ref.at[line], tile_out.at[line]).wait()
        return carry

    def finish_pack(group, carry):
        pltpu.make_async_copy(turned.at[group], pack_ref.at[group], pack_out.at[group]).wait()
        return carry

    lax.fori_loop(0, lines, fetch_gain, 0)
    lax.fori_loop(0, lines, fetch_tile, 0)
    lax.fori_loop(0, fronts * 2, turn, 0)
    lax.fori_loop(0, lines, store_tile, 0)
    lax.fori_loop(0, lines, finish_tile, 0)
    lax.fori_loop(0, fronts * 2, finish_pack, 0)


def fused_kernel(
    fronts, half_blocks, cols_each, n_sites,
    pick_ref, gain_ref, tile_ref,
    own_ref, got_ref, diag_ref,
    tile, picked, panels, prods, got, kept, d_out, d_in, parts, parts_in,
    tile_sem, own_sem, ex_send, ex_recv, side_send, side_recv,
    rs_send, rs_recv, d_send, d_recv, e_send, e_recv, put_sem, keep_sem,
):
    n_wide = lax.axis_size("wide")
    n_narrow = lax.axis_size("narrow")
    w = lax.axis_index("wide")
    n = lax.axis_index("narrow")
    right = lax.rem(w + 1, n_wide)
    left = lax.rem(w + n_wide - 1, n_wide)
    partner = 1 - n
    shards_each = n_wide // n_narrow
    width = panels.shape[3]
    site_rows = width // IMG
    slice_rows = IMG // n_wide

    tile_copy = pltpu.make_async_copy(tile_ref, tile, tile_sem)
    tile_copy.start()
    own_copies = []
    for f in range(fronts):
        own_copies.append(
            pltpu.make_async_copy(gain_ref.at[f, 0], panels.at[f, 0, 0], own_sem.at[f])
        )
        own_copies[-1].start()

    barrier = pltpu.get_barrier_semaphore()
    for step in range(1, n_wide):
        pl.semaphore_signal(
            barrier, inc=1, device_id={"wide": lax.rem(w + step, n_wide)}, device_id_type=MESH
        )
    pl.semaphore_signal(barrier, inc=1, device_id={"narrow": partner}, device_id_type=MESH)
    pl.semaphore_wait(barrier, n_wide)

    def exchange(f):
        return pltpu.make_async_remote_copy(
            src_ref=gain_ref.at[f, 1], dst_ref=panels.at[f, 0, 1],
            send_sem=ex_send.at[f], recv_sem=ex_recv.at[f],
            device_id={"narrow": partner}, device_id_type=MESH,
        )

    last = n_wide - 1

    def hop(f, h, way, hops):
        source = hops if way == 0 else (n_wide - hops) % n_wide
        target = hops + 1 if way == 0 else last - hops
        return pltpu.make_async_remote_copy(
            src_ref=panels.at[f, source, h], dst_ref=panels.at[f, target, h],
            send_sem=side_send.at[f, h, way, hops], recv_sem=side_recv.at[f, h, way, hops],
            device_id={"wide": right if way == 0 else left}, device_id_type=MESH,
        )

    def sends(way, hops):
        if way == 0:
            return (w >= hops) & (w < last)
        return (w + hops <= last) & (w > 0)

    def start_own(f, h, when=True):
        for way in range(2):
            pl.when(sends(way, 0) & when)(hop(f, h, way, 0).start)

    def forward(f, h, hops):
        for way in range(2):

            @pl.when(sends(way, hops))
            def _():
                hop(f, h, way, hops - 1).wait_recv()
                hop(f, h, way, hops).start()

    def scatter(f, d, i):
        return pltpu.make_async_remote_copy(
            src_ref=prods.at[f, d], dst_ref=got.at[f, i],
            send_sem=rs_send.at[f, i], recv_sem=rs_recv.at[f, i],
            device_id={"narrow": partner}, device_id_type=MESH,
        )

    def keep(f, d, i):
        return pltpu.make_async_copy(prods.at[f, d], own_ref.at[f, i], keep_sem.at[f, i])

    def put(f, i):
        return pltpu.make_async_copy(got.at[f, i], got_ref.at[f, i], put_sem.at[f, i])

    def swap_sites(f):
        return pltpu.make_async_remote_copy(
            src_ref=d_out.at[f], dst_ref=d_in.at[f],
            send_sem=d_send.at[f], recv_sem=d_recv.at[f],
            device_id={"narrow": partner}, device_id_type=MESH,
        )

    def spread(f, step):
        to = lax.rem(w + step, n_wide)
        return pltpu.make_async_remote_copy(
            src_ref=parts.at[f, to], dst_ref=parts_in.at[f, step - 1],
            send_sem=e_send.at[f, step - 1], recv_sem=e_recv.at[f, step - 1],
            device_id={"wide": to}, device_id_type=MESH,
        )

    side_half = jnp.where(w // shards_each == n, 0, 1)

    def choose(f, d):
        def one(t, carry):
            rows = pl.ds(pl.multiple_of(t * BLK, BLK), BLK)
            blocks = [
                panels[f, d, side_half, rows, r * BLK : (r + 1) * BLK].astype(jnp.float32)
                for r in range(half_blocks)
            ]

            def column(j, inner):
                total = pick_ref[f, j, 0] * blocks[0]
                for r in range(1, half_blocks):
                    total += pick_ref[f, j, r] * blocks[r]
                picked[rows, pl.ds(pl.multiple_of(j * BLK, BLK), BLK)] = total.astype(jnp.bfloat16)
                return inner

            return lax.fori_loop(0, cols_each, column, carry)

        lax.fori_loop(0, width // BLK, one, 0)

    def site_product(left_ref, site):
        rows = pl.ds(pl.multiple_of(site * IMG, IMG), IMG)
        return lax.dot_general(
            left_ref[rows, :], picked[rows, :], NT, preferred_element_type=jnp.float32
        )

    col_step = 256

    def compute(f, d):
        s = lax.rem(w + n_wide - d, n_wide)
        i = lax.rem(s, shards_each)
        mine = s // shards_each == n

        def one(t, carry):
            cols = pl.ds(pl.multiple_of(t * col_step, col_step), col_step)
            total = jnp.dot(
                panels[f, d, 0], tile[f, 0, :, cols], preferred_element_type=jnp.float32
            ) + jnp.dot(panels[f, d, 1], tile[f, 1, :, cols], preferred_element_type=jnp.float32)
            prods[f, d, :, cols] = total.astype(jnp.bfloat16)
            return carry

        lax.fori_loop(0, cols_each * BLK // col_step, one, 0)

        @pl.when(mine)
        def _():
            keep(f, d, i).start()

        @pl.when(jnp.logical_not(mine))
        def _():
            scatter(f, d, i).start()

        choose(f, d)

        def one_site(site, carry):
            value = site_product(prods.at[f, d], site)

            @pl.when(mine)
            def _():
                kept[f, i * site_rows + site] = value

            @pl.when(jnp.logical_not(mine))
            def _():
                d_out[f, i * site_rows + site] = value.astype(jnp.bfloat16)

            return carry

        lax.fori_loop(0, site_rows, one_site, 0)

    def absorb(f, i):
        scatter(f, 0, i).wait_recv()
        put(f, i).start()
        d = lax.rem(w + n_wide - (n * shards_each + i), n_wide)

        choose(f, d)

        def one_site(site, carry):
            value = site_product(got.at[f, i], site)
            kept[f, i * site_rows + site] += value + value.T
            return carry

        lax.fori_loop(0, site_rows, one_site, 0)

    def fold(f):
        swap_sites(f).wait_recv()

        def one_site(site, carry):
            total = (kept[f, site] + d_in[f, site].astype(jnp.float32)).astype(jnp.bfloat16)
            for z in range(n_wide):
                parts[f, z, site] = total[z * slice_rows : (z + 1) * slice_rows]
            return carry

        lax.fori_loop(0, n_sites, one_site, 0)
        for step in range(1, n_wide):
            spread(f, step).start()

    late = ((w == last - 1) & (n == n_narrow - 1)) | ((w == 1) & (n == 0))
    kept_last = lax.rem(w, shards_each) == n

    def late_own(f, h, when):
        pl.when(when & (w == last - 1))(hop(f, h, 0, 0).start)
        pl.when(when & (w == 1))(hop(f, h, 1, 0).start)

    def early_other(f, h, when):
        pl.when(when & (w == last - 1))(hop(f, h, 1, 0).start)
        pl.when(when & (w == 1))(hop(f, h, 0, 0).start)

    def others(f):
        for j in range(1, n_wide):
            k = jnp.where(kept_last, j % (n_wide - 1) + 1, j)
            for m in range(1, n_wide):
                for end, way in ((last, 0), (0, 1)):

                    @pl.when((w == end) & (k == m))
                    def _():
                        for h in range(2):
                            hop(f, h, way, m - 1).wait_recv()

            compute(f, jnp.where(w >= n_wide // 2, k, n_wide - k))
            if j == n_wide - 2:
                swap_sites(f).start()

    for f in range(fronts):
        exchange(f).start()
    for copy in own_copies:
        copy.wait()
    start_own(0, 0)
    exchange(0).wait_recv()
    start_own(0, 1)
    tile_copy.wait()
    for f in range(fronts):
        final = f == fronts - 1
        forward(f, 0, 1)
        compute(f, 0)
        forward(f, 0, 2)
        forward(f, 1, 1)
        if not final:
            exchange(f + 1).wait_recv()
            start_own(f + 1, 0)
        forward(f, 1, 2)
        if final:
            late_own(f, 1, late)
        else:
            if f + 1 == fronts - 1:
                start_own(f + 1, 1, jnp.logical_not(late))
                early_other(f + 1, 1, late)
            else:
                start_own(f + 1, 1)
        if f > 0:
            for i in range(shards_each):
                absorb(f - 1, i)
            fold(f - 1)
        others(f)
    for i in range(shards_each):
        absorb(fronts - 1, i)
    fold(fronts - 1)

    for f in range(fronts):
        for step in range(1, n_wide):
            spread(f, step).wait_recv()
        total = parts[f, w].astype(jnp.float32)
        for step in range(1, n_wide):
            total += parts_in[f, step - 1].astype(jnp.float32)
        diag_ref[f] = total

    for f in range(fronts):
        exchange(f).wait_send()
        swap_sites(f).wait_send()
        for step in range(1, n_wide):
            spread(f, step).wait_send()
        for h in range(2):
            for way in range(2):
                for hops in range(last):
                    pl.when(sends(way, hops))(hop(f, h, way, hops).wait_send)
        for i in range(shards_each):
            scatter(f, 0, i).wait_send()
            keep(f, 0, i).wait()
            put(f, i).wait()


def ranked(flags, count):
    at = jnp.cumsum(flags, axis=-1) - 1
    hit = flags[..., None, :] * (
        at[..., None, :] == jnp.arange(count, dtype=jnp.int32)[:, None]
    ).astype(jnp.int32)
    return jnp.sum(hit * jnp.arange(flags.shape[-1], dtype=jnp.int32), axis=-1)


def fused(boundary, owner, ancestor_cov, gain, pivot_inverse):
    n_wide = lax.axis_size("wide")
    n_narrow = lax.axis_size("narrow")
    w = lax.axis_index("wide")
    n = lax.axis_index("narrow")
    fronts, blocks = boundary.shape
    cols_each = blocks // n_wide
    blocks_each = blocks // n_narrow
    half_blocks = blocks_each // n_narrow
    range_blocks = ancestor_cov.shape[2] // BLK
    width = gain.shape[2]
    pivots_here = width * n_wide // n_narrow
    n_sites = pivots_here // IMG
    shards_each = n_wide // n_narrow
    slice_rows = IMG // n_wide
    bf16 = jnp.bfloat16

    holders = owner[boundary].reshape(fronts, n_narrow, blocks_each)
    own = (holders == n).astype(jnp.int32)
    places = ranked(own, half_blocks)
    mine_first = jnp.stack(
        [lax.dynamic_index_in_dim(places, n, 1, False), lax.dynamic_index_in_dim(places, 1 - n, 1, False) ],
        axis=1,
    )
    base = jnp.stack([n, 1 - n]).astype(jnp.int32)[None, :, None] * blocks_each
    at = (mine_first + base).reshape(fronts, 2 * half_blocks)
    slots = jnp.take_along_axis(boundary, at, axis=1) // n_narrow
    given = ranked(1 - lax.dynamic_index_in_dim(own, n, 1, False), half_blocks)
    take = jnp.concatenate([lax.dynamic_index_in_dim(places, n, 1, False), given], axis=1)
    columns = lax.dynamic_slice_in_dim(boundary, w * cols_each, cols_each, 1) - w * range_blocks
    columns = columns * BLK
    order = jnp.cumsum(own, axis=2) - 1
    order = order.reshape(fronts, blocks)
    ranks = lax.dynamic_slice_in_dim(order, w * cols_each, cols_each, 1)
    mask = lax.dynamic_slice_in_dim(own.reshape(fronts, blocks), w * cols_each, cols_each, 1)
    picks = mask[:, :, None] * (
        ranks[:, :, None] == jnp.arange(half_blocks, dtype=jnp.int32)
    ).astype(jnp.int32)
    picks = picks.astype(jnp.float32)

    rows = half_blocks * BLK
    cols = cols_each * BLK
    dma = pltpu.SemaphoreType.DMA
    smem = pl.BlockSpec(memory_space=pltpu.SMEM)
    anywhere = pl.BlockSpec(memory_space=pl.ANY)
    lines = fronts * 2 * half_blocks
    tile, packed = pl.pallas_call(
        functools.partial(pick_kernel, fronts, half_blocks, cols_each),
        out_shape=(
            jax.ShapeDtypeStruct((lines, BLK, cols), bf16),
            jax.ShapeDtypeStruct((fronts * 2, width, rows), bf16),
        ),
        in_specs=[smem] * 3 + [anywhere] * 2,
        out_specs=(anywhere, anywhere),
        scratch_shapes=[
            pltpu.VMEM((lines, BLK, cols), bf16),
            pltpu.VMEM((lines, BLK, width), bf16),
            pltpu.VMEM((fronts * 2, width, rows), bf16),
            dma((lines,)),
            dma((lines,)),
            dma((lines,)),
            dma((fronts * 2,)),
        ],
        compiler_params=pltpu.CompilerParams(vmem_limit_bytes=48 * 1024 * 1024),
    )(slots, columns, take, ancestor_cov, gain.reshape(lines, BLK, width))
    tile = tile.reshape(fronts, 2, rows, cols)
    packed = packed.reshape(fronts, 2, width, rows)
    piece = jax.ShapeDtypeStruct((fronts, shards_each, width, cols), bf16)
    kept_part, got_part, sites = pl.pallas_call(
        functools.partial(fused_kernel, fronts, half_blocks, cols_each, n_sites),
        out_shape=(
            piece,
            piece,
            jax.ShapeDtypeStruct((fronts, n_sites, slice_rows, IMG), jnp.float32),
        ),
        in_specs=[smem] + [anywhere] * 2,
        out_specs=(anywhere, anywhere, pl.BlockSpec(memory_space=pltpu.VMEM)),
        scratch_shapes=[
            pltpu.VMEM((fronts, 2, rows, cols), bf16),
            pltpu.VMEM((width, cols), bf16),
            pltpu.VMEM((fronts, n_wide, 2, width, rows), bf16),
            pltpu.VMEM((fronts, n_wide, width, cols), bf16),
            pltpu.VMEM((fronts, shards_each, width, cols), bf16),
            pltpu.VMEM((fronts, n_sites, IMG, IMG), jnp.float32),
            pltpu.VMEM((fronts, n_sites, IMG, IMG), bf16),
            pltpu.VMEM((fronts, n_sites, IMG, IMG), bf16),
            pltpu.VMEM((fronts, n_wide, n_sites, slice_rows, IMG), bf16),
            pltpu.VMEM((fronts, n_wide - 1, n_sites, slice_rows, IMG), bf16),
            dma,
            dma((fronts,)),
            dma((fronts,)),
            dma((fronts,)),
            dma((fronts, 2, 2, n_wide - 1)),
            dma((fronts, 2, 2, n_wide - 1)),
            dma((fronts, shards_each)),
            dma((fronts, shards_each)),
            dma((fronts,)),
            dma((fronts,)),
            dma((fronts, n_wide - 1)),
            dma((fronts, n_wide - 1)),
            dma((fronts, shards_each)),
            dma((fronts, shards_each)),
        ],
        compiler_params=pltpu.CompilerParams(
            collective_id=0, has_side_effects=True, vmem_limit_bytes=62 * 1024 * 1024
        ),
    )(picks, packed, tile)
    boundary_cov = -(kept_part.astype(jnp.float32) + got_part.astype(jnp.float32))
    boundary_cov = boundary_cov.reshape(fronts, pivots_here, cols)
    sums = jnp.swapaxes(sites, 2, 3).reshape(fronts, pivots_here, slice_rows)
    return (boundary_cov, pivot_inverse + sums)


def solution(mesh):
    placed = (
        P("front", None),
        P(),
        P("narrow", None, "wide"),
        P("front", "narrow", "wide"),
        P("front", "narrow", "wide"),
    )
    small = mesh.shape["wide"] == 4 and mesh.shape["narrow"] == 2
    return jax.shard_map(
        fused if small else local,
        mesh=mesh,
        in_specs=placed,
        out_specs=(P("front", "narrow", "wide"), P("front", "narrow", "wide")),
        check_vma=False,
    )
```

```python
import functools

import jax
import jax.numpy as jnp
from jax import lax
from jax.experimental import pallas as pl
from jax.experimental.pallas import tpu as pltpu
from jax.sharding import PartitionSpec as P

BLK = 128
IMG = 256


def slot_plan(boundary_set, owner, source, n_narrow, blocks_each, capacity):
    positions = boundary_set.reshape(n_narrow, blocks_each)
    holders = owner[positions]
    owned_mask = (holders == source).astype(jnp.int32)
    rank_of = jnp.cumsum(owned_mask, axis=1) - 1
    slot_ids = jnp.arange(capacity, dtype=jnp.int32)
    picked = owned_mask[:, None, :] * (rank_of[:, None, :] == slot_ids[None, :, None]).astype(
        jnp.int32
    )
    local_slot = jnp.sum(picked * (positions // n_narrow)[:, None, :], axis=2)
    is_valid = jnp.sum(picked, axis=2)
    return (local_slot, is_valid)


def column_panel(ancestor_cov, boundary_set, wide_index, rows_each, range_blocks):
    col_blocks = (
        lax.dynamic_slice_in_dim(boundary_set, wide_index * rows_each, rows_each)
        - wide_index * range_blocks
    )
    reshaped = ancestor_cov.reshape(ancestor_cov.shape[0], BLK, range_blocks, BLK)
    picked = jnp.take(reshaped, col_blocks, axis=2)
    return picked.reshape(ancestor_cov.shape[0], BLK, rows_each * BLK)


def arrange(arrived, boundary_set, owner, narrow, blocks_each, capacity):
    positions = lax.dynamic_slice_in_dim(boundary_set, narrow * blocks_each, blocks_each)
    holders = owner[positions]
    matches = (holders[:, None] == holders[None, :]).astype(jnp.int32)
    rank_of = jnp.sum(jnp.tril(matches, -1), axis=1)
    flattened = arrived.reshape((-1,) + arrived.shape[2:])
    chosen = jnp.take(flattened, holders * capacity + rank_of, axis=0)
    return chosen.reshape(blocks_each * chosen.shape[1], chosen.shape[2])


def local(boundary, owner, ancestor_cov, gain, pivot_inverse):
    n_wide = lax.axis_size("wide")
    n_narrow = lax.axis_size("narrow")
    wide_index = lax.axis_index("wide")
    narrow = lax.axis_index("narrow")
    fronts, blocks = boundary.shape
    rows_each = blocks // n_wide
    blocks_each = blocks // n_narrow
    range_blocks = ancestor_cov.shape[2] // BLK
    capacity = max(1, blocks_each // n_narrow)
    pivots = gain.shape[2] * n_wide
    pivots_here = pivots // n_narrow
    site_count = pivots_here // IMG
    results = []
    for member in range(fronts):
        local_slot, is_valid = slot_plan(
            boundary[member], owner, narrow, n_narrow, blocks_each, capacity
        )
        row_panel = column_panel(
            ancestor_cov, boundary[member], wide_index, rows_each, range_blocks
        )
        rows_out = jnp.take(row_panel, local_slot.reshape(-1), axis=0)
        rows_out = rows_out.reshape(n_narrow, capacity, BLK, rows_each * BLK)
        arrived = lax.all_to_all(
            jnp.where(
                is_valid.reshape(n_narrow, capacity, 1, 1) > 0, rows_out, jnp.zeros_like(rows_out)
            ),
            "narrow",
            split_axis=0,
            concat_axis=0,
            tiled=True,
        )
        coupling = arrange(arrived, boundary[member], owner, narrow, blocks_each, capacity)
        gathered = lax.all_gather(gain[member], "wide", axis=1, tiled=True)
        summed = lax.psum_scatter(
            lax.dot_general(
                gathered, coupling, (((0,), (0,)), ((), ())), preferred_element_type=jnp.float32
            ).astype(jnp.bfloat16),
            "narrow",
            scatter_dimension=0,
            tiled=True,
        ).astype(jnp.float32)
        cross_cov = -summed
        root_index = wide_index * rows_each // blocks_each
        offset = (
            jnp.clip(wide_index * rows_each - narrow * blocks_each, 0, blocks_each - rows_each)
            * BLK
        )
        own_rows = lax.dynamic_slice_in_dim(gathered, offset, rows_each * BLK, 0)
        pieces = jnp.transpose(own_rows.reshape(rows_each * BLK, n_narrow, pivots_here), (1, 0, 2))
        arrived_pieces = lax.all_to_all(pieces, "narrow", split_axis=0, concat_axis=0, tiled=True)
        gain_here = lax.dynamic_index_in_dim(arrived_pieces, root_index, 0, keepdims=False)
        cross_low = cross_cov.astype(jnp.bfloat16)
        left_side = cross_low.reshape(site_count, IMG, rows_each * BLK)
        right_side = gain_here.reshape(rows_each * BLK, site_count, IMG)
        blocks_out = jnp.einsum(
            "ipr,riq->ipq", left_side, right_side, preferred_element_type=jnp.float32
        )
        partial_value = blocks_out.reshape(pivots_here, IMG)
        reduced = lax.psum_scatter(
            partial_value.astype(jnp.bfloat16), "wide", scatter_dimension=1, tiled=True
        ).astype(jnp.float32)
        results.append((cross_cov, pivot_inverse[member] - reduced))
    boundary_cov = jnp.stack([pair[0] for pair in results])
    diag_cov = jnp.stack([pair[1] for pair in results])
    return (boundary_cov, diag_cov)


MESH = pl.DeviceIdType.MESH
NT = (((1,), (1,)), ((), ()))


def pick_kernel(
    fronts, half_blocks, cols_each,
    slot_ref, col_ref, take_ref, cov_ref, gain_ref, tile_ref, pack_ref,
    tiles, raw, turned, tile_in, raw_in, tile_out, pack_out,
):
    per_front = 2 * half_blocks
    lines = fronts * per_front

    def fetch_gain(line, carry):
        f = line // per_front
        at = f * per_front + take_ref[f, lax.rem(line, per_front)]
        pltpu.make_async_copy(gain_ref.at[at], raw.at[line], raw_in.at[line]).start()
        return carry

    def fetch_tile(line, carry):
        f = line // per_front
        slot = slot_ref[f, lax.rem(line, per_front)]
        for c in range(cols_each):
            col = pl.multiple_of(col_ref[f, c], BLK)
            pltpu.make_async_copy(
                cov_ref.at[slot, :, pl.ds(col, BLK)],
                tiles.at[line, :, pl.ds(c * BLK, BLK)],
                tile_in.at[line],
            ).start()
        return carry

    def turn(group, carry):
        for r in range(half_blocks):
            line = group * half_blocks + r
            pltpu.make_async_copy(raw.at[line], raw.at[line], raw_in.at[line]).wait()
            turned[group, :, r * BLK : (r + 1) * BLK] = raw[line].T
        pltpu.make_async_copy(turned.at[group], pack_ref.at[group], pack_out.at[group]).start()
        return carry

    def store_tile(line, carry):
        pltpu.make_async_copy(tiles.at[line], tiles.at[line], tile_in.at[line]).wait()
        pltpu.make_async_copy(tiles.at[line], tile_ref.at[line], tile_out.at[line]).start()
        return carry

    def finish_tile(line, carry):
        pltpu.make_async_copy(tiles.at[line], tile_ref.at[line], tile_out.at[line]).wait()
        return carry

    def finish_pack(group, carry):
        pltpu.make_async_copy(turned.at[group], pack_ref.at[group], pack_out.at[group]).wait()
        return carry

    lax.fori_loop(0, lines, fetch_gain, 0)
    lax.fori_loop(0, lines, fetch_tile, 0)
    lax.fori_loop(0, fronts * 2, turn, 0)
    lax.fori_loop(0, lines, store_tile, 0)
    lax.fori_loop(0, lines, finish_tile, 0)
    lax.fori_loop(0, fronts * 2, finish_pack, 0)


def fused_kernel(
    fronts, half_blocks, cols_each, n_sites,
    pick_ref, gain_ref, tile_ref,
    own_ref, got_ref, diag_ref,
    tile, picked, panels, prods, got, kept, d_out, d_in, parts, parts_in,
    tile_sem, own_sem, ex_send, ex_recv, side_send, side_recv,
    rs_send, rs_recv, d_send, d_recv, e_send, e_recv, put_sem, keep_sem,
):
    n_wide = lax.axis_size("wide")
    n_narrow = lax.axis_size("narrow")
    w = lax.axis_index("wide")
    n = lax.axis_index("narrow")
    right = lax.rem(w + 1, n_wide)
    left = lax.rem(w + n_wide - 1, n_wide)
    partner = 1 - n
    shards_each = n_wide // n_narrow
    width = panels.shape[3]
    site_rows = width // IMG
    slice_rows = IMG // n_wide

    tile_copy = pltpu.make_async_copy(tile_ref, tile, tile_sem)
    tile_copy.start()
    own_copies = []
    for f in range(fronts):
        own_copies.append(
            pltpu.make_async_copy(gain_ref.at[f, 0], panels.at[f, 0, 0], own_sem.at[f])
        )
        own_copies[-1].start()

    barrier = pltpu.get_barrier_semaphore()
    for step in range(1, n_wide):
        pl.semaphore_signal(
            barrier, inc=1, device_id={"wide": lax.rem(w + step, n_wide)}, device_id_type=MESH
        )
    pl.semaphore_signal(barrier, inc=1, device_id={"narrow": partner}, device_id_type=MESH)
    pl.semaphore_wait(barrier, n_wide)

    def exchange(f):
        return pltpu.make_async_remote_copy(
            src_ref=gain_ref.at[f, 1], dst_ref=panels.at[f, 0, 1],
            send_sem=ex_send.at[f], recv_sem=ex_recv.at[f],
            device_id={"narrow": partner}, device_id_type=MESH,
        )

    last = n_wide - 1

    def hop(f, h, way, hops):
        source = hops if way == 0 else (n_wide - hops) % n_wide
        target = hops + 1 if way == 0 else last - hops
        return pltpu.make_async_remote_copy(
            src_ref=panels.at[f, source, h], dst_ref=panels.at[f, target, h],
            send_sem=side_send.at[f, h, way, hops], recv_sem=side_recv.at[f, h, way, hops],
            device_id={"wide": right if way == 0 else left}, device_id_type=MESH,
        )

    def sends(way, hops):
        if way == 0:
            return (w >= hops) & (w < last)
        return (w + hops <= last) & (w > 0)

    def start_own(f, h, when=True):
        for way in range(2):
            pl.when(sends(way, 0) & when)(hop(f, h, way, 0).start)

    def forward(f, h, hops):
        for way in range(2):

            @pl.when(sends(way, hops))
            def _():
                hop(f, h, way, hops - 1).wait_recv()
                hop(f, h, way, hops).start()

    def scatter(f, d, i):
        return pltpu.make_async_remote_copy(
            src_ref=prods.at[f, d], dst_ref=got.at[f, i],
            send_sem=rs_send.at[f, i], recv_sem=rs_recv.at[f, i],
            device_id={"narrow": partner}, device_id_type=MESH,
        )

    def keep(f, d, i):
        return pltpu.make_async_copy(prods.at[f, d], own_ref.at[f, i], keep_sem.at[f, i])

    def put(f, i):
        return pltpu.make_async_copy(got.at[f, i], got_ref.at[f, i], put_sem.at[f, i])

    def swap_sites(f):
        return pltpu.make_async_remote_copy(
            src_ref=d_out.at[f], dst_ref=d_in.at[f],
            send_sem=d_send.at[f], recv_sem=d_recv.at[f],
            device_id={"narrow": partner}, device_id_type=MESH,
        )

    def spread(f, step):
        to = lax.rem(w + step, n_wide)
        return pltpu.make_async_remote_copy(
            src_ref=parts.at[f, to], dst_ref=parts_in.at[f, step - 1],
            send_sem=e_send.at[f, step - 1], recv_sem=e_recv.at[f, step - 1],
            device_id={"wide": to}, device_id_type=MESH,
        )

    side_half = jnp.where(w // shards_each == n, 0, 1)

    def choose(f, d):
        def one(t, carry):
            rows = pl.ds(pl.multiple_of(t * BLK, BLK), BLK)
            blocks = [
                panels[f, d, side_half, rows, r * BLK : (r + 1) * BLK].astype(jnp.float32)
                for r in range(half_blocks)
            ]

            def column(j, inner):
                total = pick_ref[f, j, 0] * blocks[0]
                for r in range(1, half_blocks):
                    total += pick_ref[f, j, r] * blocks[r]
                picked[rows, pl.ds(pl.multiple_of(j * BLK, BLK), BLK)] = total.astype(jnp.bfloat16)
                return inner

            return lax.fori_loop(0, cols_each, column, carry)

        lax.fori_loop(0, width // BLK, one, 0)

    def site_product(left_ref, site):
        rows = pl.ds(pl.multiple_of(site * IMG, IMG), IMG)
        return lax.dot_general(
            left_ref[rows, :], picked[rows, :], NT, preferred_element_type=jnp.float32
        )

    col_step = 256

    def compute(f, d):
        s = lax.rem(w + n_wide - d, n_wide)
        i = lax.rem(s, shards_each)
        mine = s // shards_each == n

        def one(t, carry):
            cols = pl.ds(pl.multiple_of(t * col_step, col_step), col_step)
            total = jnp.dot(
                panels[f, d, 0], tile[f, 0, :, cols], preferred_element_type=jnp.float32
            ) + jnp.dot(panels[f, d, 1], tile[f, 1, :, cols], preferred_element_type=jnp.float32)
            prods[f, d, :, cols] = total.astype(jnp.bfloat16)
            return carry

        lax.fori_loop(0, cols_each * BLK // col_step, one, 0)

        @pl.when(mine)
        def _():
            keep(f, d, i).start()

        @pl.when(jnp.logical_not(mine))
        def _():
            scatter(f, d, i).start()

        choose(f, d)

        def one_site(site, carry):
            value = site_product(prods.at[f, d], site)

            @pl.when(mine)
            def _():
                kept[f, i * site_rows + site] = value

            @pl.when(jnp.logical_not(mine))
            def _():
                d_out[f, i * site_rows + site] = value.astype(jnp.bfloat16)

            return carry

        lax.fori_loop(0, site_rows, one_site, 0)

    def absorb(f, i):
        scatter(f, 0, i).wait_recv()
        put(f, i).start()
        d = lax.rem(w + n_wide - (n * shards_each + i), n_wide)

        choose(f, d)

        def one_site(site, carry):
            value = site_product(got.at[f, i], site)
            kept[f, i * site_rows + site] += value + value.T
            return carry

        lax.fori_loop(0, site_rows, one_site, 0)

    def fold(f):
        swap_sites(f).wait_recv()

        def one_site(site, carry):
            total = (kept[f, site] + d_in[f, site].astype(jnp.float32)).astype(jnp.bfloat16)
            for z in range(n_wide):
                parts[f, z, site] = total[z * slice_rows : (z + 1) * slice_rows]
            return carry

        lax.fori_loop(0, n_sites, one_site, 0)
        for step in range(1, n_wide):
            spread(f, step).start()

    late = ((w == last - 1) & (n == n_narrow - 1)) | ((w == 1) & (n == 0))
    kept_last = lax.rem(w, shards_each) == n

    def late_own(f, h, when):
        pl.when(when & (w == last - 1))(hop(f, h, 0, 0).start)
        pl.when(when & (w == 1))(hop(f, h, 1, 0).start)

    def early_other(f, h, when):
        pl.when(when & (w == last - 1))(hop(f, h, 1, 0).start)
        pl.when(when & (w == 1))(hop(f, h, 0, 0).start)

    def others(f):
        for j in range(1, n_wide):
            k = jnp.where(kept_last, j % (n_wide - 1) + 1, j)
            for m in range(1, n_wide):
                for end, way in ((last, 0), (0, 1)):

                    @pl.when((w == end) & (k == m))
                    def _():
                        for h in range(2):
                            hop(f, h, way, m - 1).wait_recv()

            compute(f, jnp.where(w >= n_wide // 2, k, n_wide - k))
            if j == n_wide - 2:
                swap_sites(f).start()

    for f in range(fronts):
        exchange(f).start()
    own_copies[0].wait()
    start_own(0, 0)
    for copy in own_copies[1:]:
        copy.wait()
    if fronts > 1:
        start_own(1, 0)
    exchange(0).wait_recv()
    start_own(0, 1)
    tile_copy.wait()
    for f in range(fronts):
        final = f == fronts - 1
        forward(f, 0, 1)
        compute(f, 0)
        forward(f, 0, 2)
        forward(f, 1, 1)
        if not final:
            exchange(f + 1).wait_recv()
            if f > 0:
                start_own(f + 1, 0)
        forward(f, 1, 2)
        if final:
            late_own(f, 1, late)
        else:
            if f + 1 == fronts - 1:
                start_own(f + 1, 1, jnp.logical_not(late))
                early_other(f + 1, 1, late)
            else:
                start_own(f + 1, 1)
        if f > 0:
            for i in range(shards_each):
                absorb(f - 1, i)
            fold(f - 1)
        others(f)
    for i in range(shards_each):
        absorb(fronts - 1, i)
    fold(fronts - 1)

    for f in range(fronts):
        for step in range(1, n_wide):
            spread(f, step).wait_recv()
        total = parts[f, w].astype(jnp.float32)
        for step in range(1, n_wide):
            total += parts_in[f, step - 1].astype(jnp.float32)
        diag_ref[f] = total

    for f in range(fronts):
        exchange(f).wait_send()
        swap_sites(f).wait_send()
        for step in range(1, n_wide):
            spread(f, step).wait_send()
        for h in range(2):
            for way in range(2):
                for hops in range(last):
                    pl.when(sends(way, hops))(hop(f, h, way, hops).wait_send)
        for i in range(shards_each):
            scatter(f, 0, i).wait_send()
            keep(f, 0, i).wait()
            put(f, i).wait()


def ranked(flags, count):
    at = jnp.cumsum(flags, axis=-1) - 1
    hit = flags[..., None, :] * (
        at[..., None, :] == jnp.arange(count, dtype=jnp.int32)[:, None]
    ).astype(jnp.int32)
    return jnp.sum(hit * jnp.arange(flags.shape[-1], dtype=jnp.int32), axis=-1)


def fused(boundary, owner, ancestor_cov, gain, pivot_inverse):
    n_wide = lax.axis_size("wide")
    n_narrow = lax.axis_size("narrow")
    w = lax.axis_index("wide")
    n = lax.axis_index("narrow")
    fronts, blocks = boundary.shape
    cols_each = blocks // n_wide
    blocks_each = blocks // n_narrow
    half_blocks = blocks_each // n_narrow
    range_blocks = ancestor_cov.shape[2] // BLK
    width = gain.shape[2]
    pivots_here = width * n_wide // n_narrow
    n_sites = pivots_here // IMG
    shards_each = n_wide // n_narrow
    slice_rows = IMG // n_wide
    bf16 = jnp.bfloat16

    holders = owner[boundary].reshape(fronts, n_narrow, blocks_each)
    own = (holders == n).astype(jnp.int32)
    places = ranked(own, half_blocks)
    mine_first = jnp.stack(
        [lax.dynamic_index_in_dim(places, n, 1, False), lax.dynamic_index_in_dim(places, 1 - n, 1, False) ],
        axis=1,
    )
    base = jnp.stack([n, 1 - n]).astype(jnp.int32)[None, :, None] * blocks_each
    at = (mine_first + base).reshape(fronts, 2 * half_blocks)
    slots = jnp.take_along_axis(boundary, at, axis=1) // n_narrow
    given = ranked(1 - lax.dynamic_index_in_dim(own, n, 1, False), half_blocks)
    take = jnp.concatenate([lax.dynamic_index_in_dim(places, n, 1, False), given], axis=1)
    columns = lax.dynamic_slice_in_dim(boundary, w * cols_each, cols_each, 1) - w * range_blocks
    columns = columns * BLK
    order = jnp.cumsum(own, axis=2) - 1
    order = order.reshape(fronts, blocks)
    ranks = lax.dynamic_slice_in_dim(order, w * cols_each, cols_each, 1)
    mask = lax.dynamic_slice_in_dim(own.reshape(fronts, blocks), w * cols_each, cols_each, 1)
    picks = mask[:, :, None] * (
        ranks[:, :, None] == jnp.arange(half_blocks, dtype=jnp.int32)
    ).astype(jnp.int32)
    picks = picks.astype(jnp.float32)

    rows = half_blocks * BLK
    cols = cols_each * BLK
    dma = pltpu.SemaphoreType.DMA
    smem = pl.BlockSpec(memory_space=pltpu.SMEM)
    anywhere = pl.BlockSpec(memory_space=pl.ANY)
    lines = fronts * 2 * half_blocks
    tile, packed = pl.pallas_call(
        functools.partial(pick_kernel, fronts, half_blocks, cols_each),
        out_shape=(
            jax.ShapeDtypeStruct((lines, BLK, cols), bf16),
            jax.ShapeDtypeStruct((fronts * 2, width, rows), bf16),
        ),
        in_specs=[smem] * 3 + [anywhere] * 2,
        out_specs=(anywhere, anywhere),
        scratch_shapes=[
            pltpu.VMEM((lines, BLK, cols), bf16),
            pltpu.VMEM((lines, BLK, width), bf16),
            pltpu.VMEM((fronts * 2, width, rows), bf16),
            dma((lines,)),
            dma((lines,)),
            dma((lines,)),
            dma((fronts * 2,)),
        ],
        compiler_params=pltpu.CompilerParams(vmem_limit_bytes=48 * 1024 * 1024),
    )(slots, columns, take, ancestor_cov, gain.reshape(lines, BLK, width))
    tile = tile.reshape(fronts, 2, rows, cols)
    packed = packed.reshape(fronts, 2, width, rows)
    piece = jax.ShapeDtypeStruct((fronts, shards_each, width, cols), bf16)
    kept_part, got_part, sites = pl.pallas_call(
        functools.partial(fused_kernel, fronts, half_blocks, cols_each, n_sites),
        out_shape=(
            piece,
            piece,
            jax.ShapeDtypeStruct((fronts, n_sites, slice_rows, IMG), jnp.float32),
        ),
        in_specs=[smem] + [anywhere] * 2,
        out_specs=(anywhere, anywhere, pl.BlockSpec(memory_space=pltpu.VMEM)),
        scratch_shapes=[
            pltpu.VMEM((fronts, 2, rows, cols), bf16),
            pltpu.VMEM((width, cols), bf16),
            pltpu.VMEM((fronts, n_wide, 2, width, rows), bf16),
            pltpu.VMEM((fronts, n_wide, width, cols), bf16),
            pltpu.VMEM((fronts, shards_each, width, cols), bf16),
            pltpu.VMEM((fronts, n_sites, IMG, IMG), jnp.float32),
            pltpu.VMEM((fronts, n_sites, IMG, IMG), bf16),
            pltpu.VMEM((fronts, n_sites, IMG, IMG), bf16),
            pltpu.VMEM((fronts, n_wide, n_sites, slice_rows, IMG), bf16),
            pltpu.VMEM((fronts, n_wide - 1, n_sites, slice_rows, IMG), bf16),
            dma,
            dma((fronts,)),
            dma((fronts,)),
            dma((fronts,)),
            dma((fronts, 2, 2, n_wide - 1)),
            dma((fronts, 2, 2, n_wide - 1)),
            dma((fronts, shards_each)),
            dma((fronts, shards_each)),
            dma((fronts,)),
            dma((fronts,)),
            dma((fronts, n_wide - 1)),
            dma((fronts, n_wide - 1)),
            dma((fronts, shards_each)),
            dma((fronts, shards_each)),
        ],
        compiler_params=pltpu.CompilerParams(
            collective_id=0, has_side_effects=True, vmem_limit_bytes=62 * 1024 * 1024
        ),
    )(picks, packed, tile)
    boundary_cov = -(kept_part.astype(jnp.float32) + got_part.astype(jnp.float32))
    boundary_cov = boundary_cov.reshape(fronts, pivots_here, cols)
    sums = jnp.swapaxes(sites, 2, 3).reshape(fronts, pivots_here, slice_rows)
    return (boundary_cov, pivot_inverse + sums)


def solution(mesh):
    placed = (
        P("front", None),
        P(),
        P("narrow", None, "wide"),
        P("front", "narrow", "wide"),
        P("front", "narrow", "wide"),
    )
    small = mesh.shape["wide"] == 4 and mesh.shape["narrow"] == 2
    return jax.shard_map(
        fused if small else local,
        mesh=mesh,
        in_specs=placed,
        out_specs=(P("front", "narrow", "wide"), P("front", "narrow", "wide")),
        check_vma=False,
    )
```
